256 devices in a mesh: mem: 32 (over y, x, core), col: 8 (over z).
Axes of the slice: x: 4, y: 4, z: 8, core: 2. Of those that a mesh axis runs over, the one named last changes fastest.
Arguments:
- background_trials: bfloat16 [256, 4, 128, 1024], P('mem', None, None, 'col'), may hold values from -6 to 6
- region_active_tally: int32 [32, 32], P('mem', 'col'), may hold values from 256 to 2048, as said below
- sensed_component: int32 [32, 32, 2048], P('mem', 'col'), may hold values from 0 to 1919
- distance_bucket: int32 [32, 32, 2048], P('mem', 'col'), may hold values from 0 to 15
- sensor_readings: float32 [32, 32, 2048], P('mem', 'col'), may hold values from -6 to 6
- inverse_noise_variance: float32 [32, 32, 2048], P('mem', 'col'), may hold values from 0.25 to 4
- localization_factors: float32 [16], replicated, may hold values from 0.05 to 1
Outputs:
- analysis: bfloat16 [256, 4, 128, 1024], P('mem', None, None, 'col')
The draws below stay inside these ranges and needn't reach their ends.
Inputs may be any that keep to these rules, and one draw needn't show every extreme that they name: `region_active_tally`: observations of a patch fill its first slots; some patch has exactly 2048 live observations. `sensed_component`: window entry in the order given in the reference program.
All inputs are finite; a program needn't handle non-finite values.
Results may differ from the reference program's by a relative error of at most 0.0063.
Values may be sent and summed in bfloat16 or wider, within the bound.
A program may use at most 64 MiB of HBM per device.

```python
import math
import jax
import jax.numpy as jnp
from jax import lax

NUMBER_OF_RUNS = 256
VERTICAL_UNKNOWNS = 4
STRIP_DEPTH = 4
SECTOR_SPAN = 32
REACH_MARGIN = 4
OBS = 2048
CLASSES = 16
ITERS = 4
LATITUDE_LINES = 128
LONGITUDE_LINES = 1024
NPY = 32
NPX = 32


def draw_region_active_tally(key, part):
    first_key, second_key, third_key = jax.random.split(jax.random.fold_in(key, 11), 3)
    base_count = jax.random.randint(first_key, (NPY * NPX,), OBS // 8, OBS // 2 + 1)
    is_busy = jax.random.randint(second_key, (NPY * NPX,), 0, 8) == 0
    full_spot = jax.random.randint(third_key, (), 0, NPY * NPX)
    is_full = jnp.logical_or(is_busy, jnp.arange(NPY * NPX, dtype=jnp.int32) == full_spot)
    counts_all = jnp.where(is_full, OBS, base_count)
    return counts_all.reshape(NPY, NPX).astype(jnp.int32)


def touch_ends(values, rng, least, high):
    longest = values.shape.index(max(values.shape))
    spots = []
    for shift in (0, 1):
        where = [jax.random.randint(jax.random.fold_in(rng, axis), (), 0, length) for axis, length in enumerate(values.shape)]
        where[longest] = (where[longest] + shift) % values.shape[longest]
        spots.append(tuple(where))
    return values.at[spots[0]].set(least).at[spots[1]].set(high)


def block_scale(stream_key, dims, cuts, least, largest):
    gain = 1.0
    for position, blocks in cuts:
        heights = jax.random.uniform(jax.random.fold_in(jax.random.fold_in(stream_key, 6), position), (blocks,), jnp.float32, least / len(cuts), largest / len(cuts))
        gain = gain * jnp.repeat(jnp.exp(heights), dims[position] // blocks).reshape((-1,) + (1,) * (len(dims) - 1 - position))
    return gain


def centred(key, shape, spread, bound, cuts=(), held_as=jnp.bfloat16):
    array = spread * jax.random.normal(key, shape, jnp.float32)
    if cuts:
        array = array * block_scale(key, shape, cuts, -0.22, 0.18)
    return jnp.clip(array, -bound, bound).astype(held_as)


def setup_inputs(seed: int = 0) -> dict:
    streams_of = jax.random.split(jax.random.key(seed), 8)
    background_trials = centred(streams_of[0], (NUMBER_OF_RUNS, VERTICAL_UNKNOWNS, LATITUDE_LINES, LONGITUDE_LINES), 1.0, 6.0, ((0, 32), (3, 8)))
    region_active_tally = draw_region_active_tally(jax.random.fold_in(streams_of[7], 71), 0)
    sensed_component = touch_ends(jax.random.randint(streams_of[2], (NPY, NPX, OBS), 0, VERTICAL_UNKNOWNS * (STRIP_DEPTH + 2 * REACH_MARGIN) * (SECTOR_SPAN + 2 * REACH_MARGIN)), jax.random.fold_in(streams_of[2], 1), 0, (VERTICAL_UNKNOWNS * (STRIP_DEPTH + 2 * REACH_MARGIN) * (SECTOR_SPAN + 2 * REACH_MARGIN)) - 1).astype(jnp.int32)
    distance_bucket = touch_ends(jax.random.randint(streams_of[3], (NPY, NPX, OBS), 0, CLASSES), jax.random.fold_in(streams_of[3], 1), 0, CLASSES - 1).astype(jnp.int32)
    sensor_readings = centred(streams_of[4], (NPY, NPX, OBS), 1.0, 6.0, ((0, 32), (1, 8)), jnp.float32)
    inverse_noise_variance = jnp.clip(jnp.exp(math.log(4.0) - 2.7725887 * jax.random.uniform(streams_of[5], (NPY, NPX, OBS), jnp.float32) ** block_scale(streams_of[5], (NPY, NPX, OBS), ((0, 32), (1, 8)), -0.2, 0.2)), 0.25, 4.0)
    localization_factors = jnp.clip(jnp.exp(jax.random.uniform(streams_of[6], (CLASSES,), jnp.float32, math.log(0.05), math.log(1.0))), 0.05, 1.0)
    return {"background_trials": background_trials, "region_active_tally": region_active_tally, "sensed_component": sensed_component, "distance_bucket": distance_bucket, "sensor_readings": sensor_readings, "inverse_noise_variance": inverse_noise_variance, "localization_factors": localization_factors}


inflation = 1.1

def lookup(class_ids, weight_table):
    table_slots = jnp.arange(weight_table.shape[0], dtype=jnp.int32)
    return lax.optimization_barrier(jnp.sum(jnp.where(class_ids[..., None] == table_slots, weight_table, 0.0), axis=-1))

def analyse_patch(viewing_frame, window_average, live_count, cell_ids, class_ids, values, inv_var, weight_table):
    trial_flattened = viewing_frame.shape[0]
    physical_quantity_stack = viewing_frame.shape[1]
    deviation_matrix = (viewing_frame.astype(jnp.float32) - window_average).astype(jnp.bfloat16)
    flattened = deviation_matrix.reshape(trial_flattened, -1)
    observed = jnp.take(flattened, cell_ids, axis=1)
    innovation = values - jnp.take(window_average.reshape(-1), cell_ids)
    is_live = jnp.arange(cell_ids.shape[0], dtype=jnp.int32) < live_count
    weight = jnp.where(is_live, inv_var * lookup(class_ids, weight_table), 0.0)
    scaled = (observed.astype(jnp.float32) * weight).astype(jnp.bfloat16)
    gram_sum = jnp.dot(scaled, observed.T, preferred_element_type=jnp.float32)
    forcing = jnp.dot(scaled.astype(jnp.float32), innovation, precision=lax.Precision.HIGHEST)
    identity = jnp.eye(trial_flattened, dtype=jnp.float32)
    gram_sum = gram_sum + (trial_flattened - 1) / inflation * identity
    norm_scale = jnp.sqrt(jnp.sum(gram_sum * gram_sum))
    iterate = gram_sum / norm_scale
    inverse_root = identity
    for sweep_id in range(ITERS):
        factor = 1.5 * identity - 0.5 * jnp.dot(inverse_root, iterate, precision=lax.Precision.HIGHEST)
        iterate = jnp.dot(iterate, factor, precision=lax.Precision.HIGHEST)
        inverse_root = jnp.dot(factor, inverse_root, precision=lax.Precision.HIGHEST)
    partial_shift = jnp.dot(inverse_root, forcing, precision=lax.Precision.HIGHEST)
    mean_shift = jnp.dot(inverse_root, partial_shift, precision=lax.Precision.HIGHEST) / norm_scale
    transform = jnp.sqrt((trial_flattened - 1.0) / norm_scale) * inverse_root + mean_shift[:, None]
    transform = transform.astype(jnp.bfloat16)
    own_anomaly = deviation_matrix[:, :, REACH_MARGIN:REACH_MARGIN + STRIP_DEPTH, REACH_MARGIN:REACH_MARGIN + SECTOR_SPAN].reshape(trial_flattened, -1)
    inner_midpoint = window_average[:, REACH_MARGIN:REACH_MARGIN + STRIP_DEPTH, REACH_MARGIN:REACH_MARGIN + SECTOR_SPAN].reshape(-1)
    result = jnp.dot(transform.T, own_anomaly, preferred_element_type=jnp.float32) + inner_midpoint
    return result.astype(jnp.bfloat16).reshape(trial_flattened, physical_quantity_stack, STRIP_DEPTH, SECTOR_SPAN)

def reference(background_trials, region_active_tally, sensed_component, distance_bucket, sensor_readings, inverse_noise_variance, localization_factors):
    trial_flattened, physical_quantity_stack, latitude_sum, longitude_sum = background_trials.shape
    predicted_average = lax.optimization_barrier(jnp.sum(background_trials, axis=0, dtype=jnp.float32)) / trial_flattened
    margined_predictions = jnp.pad(background_trials, ((0, 0), (0, 0), (REACH_MARGIN, REACH_MARGIN), (REACH_MARGIN, REACH_MARGIN)))
    enlarged_midpoint = jnp.pad(predicted_average, ((0, 0), (REACH_MARGIN, REACH_MARGIN), (REACH_MARGIN, REACH_MARGIN)))
    patch_cols = longitude_sum // SECTOR_SPAN
    patch_total = latitude_sum // STRIP_DEPTH * patch_cols

    def one_patch(patch_index):
        row_id = patch_index // patch_cols
        col_id = patch_index % patch_cols
        topmost_offset = (row_id * STRIP_DEPTH).astype(jnp.int32)
        leftmost_offset = (col_id * SECTOR_SPAN).astype(jnp.int32)
        corner_point = jnp.zeros((), jnp.int32)
        viewing_frame = lax.dynamic_slice(margined_predictions, (corner_point, corner_point, topmost_offset, leftmost_offset), (trial_flattened, physical_quantity_stack, STRIP_DEPTH + 2 * REACH_MARGIN, SECTOR_SPAN + 2 * REACH_MARGIN))
        window_average = lax.dynamic_slice(enlarged_midpoint, (corner_point, topmost_offset, leftmost_offset), (physical_quantity_stack, STRIP_DEPTH + 2 * REACH_MARGIN, SECTOR_SPAN + 2 * REACH_MARGIN))
        return analyse_patch(viewing_frame, window_average, region_active_tally[row_id, col_id], sensed_component[row_id, col_id], distance_bucket[row_id, col_id], sensor_readings[row_id, col_id], inverse_noise_variance[row_id, col_id], localization_factors)
    blocks = lax.map(one_patch, jnp.arange(patch_total, dtype=jnp.int32))
    blocks = blocks.reshape(latitude_sum // STRIP_DEPTH, patch_cols, trial_flattened, physical_quantity_stack, STRIP_DEPTH, SECTOR_SPAN)
    return blocks.transpose(2, 3, 0, 4, 1, 5).reshape(trial_flattened, physical_quantity_stack, latitude_sum, longitude_sum)
```

```python
import functools

import jax
import jax.numpy as jnp
from jax import lax
from jax.experimental import pallas as pl
from jax.experimental.pallas import tpu as pltpu
from jax.sharding import PartitionSpec as P

MESH = pl.DeviceIdType.MESH
F32 = jnp.float32
BF16 = jnp.bfloat16
N = 32
inflation = 1.1
members = 256


def iota(shape, dim):
    return lax.broadcasted_iota(jnp.int32, shape, dim)


def dot(a, b):
    return lax.dot_general(a, b, (((1,), (0,)), ((), ())), preferred_element_type=F32)


def dot_nt(a, b):
    return lax.dot_general(a, b, (((1,), (1,)), ((), ())), preferred_element_type=F32)


def split2(a):
    hi = a.astype(BF16)
    return hi, (a - hi.astype(F32)).astype(BF16)


def split3(a):
    hi = a.astype(BF16)
    rest = a - hi.astype(F32)
    mid = rest.astype(BF16)
    return hi, mid, (rest - mid.astype(F32)).astype(BF16)


def dot3(a, b):
    (ah, al), (bh, bl) = a, b
    return dot(
        jnp.concatenate([ah, ah, al], axis=1), jnp.concatenate([bh, bl, bh], axis=0)
    )


def swap_matrix():
    row, col = iota((512, 512), 0), iota((512, 512), 1)
    swapped = (col // 128) * 32 + ((col % 128) // 32) * 128 + col % 32
    return (row == swapped).astype(F32).astype(BF16)


def place(m):
    return (m // 8) * 2 + m % 2, (m // 2) % 4


def device_of(g, b):
    return (g // 2) * 8 + b * 2 + g % 2


def histogram(me, z, counts, cells, classes, readings, inv_var, table, out_ref):
    e = cells[...]
    s = (e >= 480).astype(jnp.int32) + (e >= 960).astype(jnp.int32) + (e >= 1440).astype(jnp.int32)
    rest = e - s * 480
    r = (rest * 1639) // 65536
    c = rest - r * 40
    dt = r // 4
    left, right = c < 4, c >= 36
    side = left | right
    slab = dt * 5 + jnp.where(side, 4, s)
    lane = jnp.where(
        side,
        jnp.where(right, 64, 0) + s * 16 + (r % 4) * 4 + c % 4,
        (r % 4) * 32 + c - 4,
    )
    column = z * 4 + iota(e.shape, 0)
    outside = (
        ((dt == 0) & (me == 0))
        | ((dt == 2) & (me == N - 1))
        | (left & (column == 0))
        | (right & (column == 31))
    )
    kind = classes[...]
    factor = jnp.zeros(e.shape, F32)
    for i in range(16):
        factor = jnp.where(kind == i, table[i], factor)
    live = (iota(e.shape, 1) < counts[...]) & ~outside
    weight = jnp.where(live, inv_var[...] * factor, 0.0)
    product = weight * readings[...]
    w_parts, v_parts = split3(weight), split3(product)
    for b in range(4):
        lanes = (iota((128, 2048), 0) == lane[b : b + 1]).astype(F32).astype(BF16)
        here = iota((16, 2048), 0) == slab[b : b + 1]
        rows = [
            jnp.where(here, part[b : b + 1].astype(F32), 0.0).astype(BF16)
            for part in w_parts + v_parts
        ]
        sums = dot_nt(jnp.concatenate(rows, axis=0), lanes)
        out_ref[b, 0] = sums[0:16] + sums[16:32] + sums[32:48]
        out_ref[b, 1] = sums[48:64] + sums[64:80] + sums[80:96]


def spread_kernel(
    x_ref, counts, cells, classes, readings, inv_var, table,
    tiles_ref, sums_ref,
    packed, mine, edge, edge_in,
    send, recv, edge_send, edge_recv, sums_send, sums_recv, halo_send, halo_recv,
):
    me = lax.axis_index("mem")
    z = lax.axis_index("col")
    g, b_me = place(me)
    barrier = pltpu.get_barrier_semaphore()

    def greet(i, carry):
        pl.semaphore_signal(
            barrier, inc=1, device_id={"mem": lax.rem(me + i, N)}, device_id_type=MESH
        )
        return carry

    lax.fori_loop(1, N, greet, 0)
    z_sides = (lax.rem(z + 1, 8), lax.rem(z + 7, 8))
    for other in z_sides:
        pl.semaphore_signal(barrier, inc=1, device_id={"col": other}, device_id_type=MESH)
    pl.semaphore_wait(barrier, N + 1)

    row, col = iota((128, 128), 0), iota((128, 128), 1)
    edge_pick = row == jnp.where(col < 64, 124, 0) + col % 4
    edges = jnp.zeros((256, 128), F32)
    for sr in range(16):
        pick = (edge_pick & ((col // 4) % 16 == sr)).astype(F32).astype(BF16)
        edges = edges + dot(x_ref[sr], pick)
    edge[...] = edges.astype(BF16)
    edge_copies = []
    for k, other in enumerate(z_sides):
        copy = pltpu.make_async_remote_copy(
            src_ref=edge, dst_ref=edge_in.at[k], send_sem=edge_send.at[k],
            recv_sem=edge_recv.at[k], device_id={"col": other}, device_id_type=MESH,
        )
        copy.start()
        edge_copies.append(copy)

    def send_slab(s):
        rows = pl.ds(pl.multiple_of(me * 8, 8), 8)
        pltpu.make_async_copy(
            packed.at[s, b_me * 8 + g], tiles_ref.at[pl.ds(1, 4), s, rows], recv.at[s]
        ).start()

        def one(i, carry):
            to = lax.rem(me + i, N)
            g_to, b_to = place(to)
            pltpu.make_async_remote_copy(
                src_ref=packed.at[s, b_to * 8 + g_to],
                dst_ref=tiles_ref.at[pl.ds(1, 4), s, rows],
                send_sem=send.at[s], recv_sem=recv.at[s],
                device_id={"mem": to}, device_id_type=MESH,
            ).start()
            return carry

        lax.fori_loop(1, N, one, 0)

    swap = swap_matrix()
    for s in range(4):
        wide = jnp.concatenate([x_ref[4 * s + r] for r in range(4)], axis=1)
        out = dot(wide, swap).astype(BF16)
        for b in range(4):
            packed[s, 8 * b : 8 * b + 8] = out[:, 128 * b : 128 * b + 128].reshape(8, 4, 8, 128)
        send_slab(s)

    row, col = iota((128, 512), 0), iota((128, 512), 1)
    side_pick = row == (col // 128) * 32 + jnp.where(col % 128 < 64, -4, 32) + col % 4
    sides = jnp.zeros((256, 512), F32)
    for sr in range(16):
        pick = (side_pick & ((col // 4) % 16 == sr)).astype(F32).astype(BF16)
        sides = sides + dot(x_ref[sr], pick)
    for copy in edge_copies:
        copy.wait()
    lane = iota((256, 128), 1)
    for b in range(4):
        part = sides[:, 128 * b : 128 * b + 128]
        if b == 0:
            part = part + jnp.where(lane < 64, edge_in[0].astype(F32), 0.0)
        if b == 3:
            part = part + jnp.where(lane < 64, 0.0, edge_in[1].astype(F32))
        packed[4, 8 * b : 8 * b + 8] = part.astype(BF16).reshape(8, 4, 8, 128)
    send_slab(4)

    histogram(me, z, counts, cells, classes, readings, inv_var, table, mine)
    for b in range(4):
        to = device_of(me // 4, b)

        def sums_copy():
            return pltpu.make_async_remote_copy(
                src_ref=mine.at[b], dst_ref=sums_ref.at[lax.rem(me, 4)],
                send_sem=sums_send.at[b], recv_sem=sums_recv,
                device_id={"mem": to}, device_id_type=MESH,
            )

        @pl.when(to != me)
        def _():
            sums_copy().start()

        @pl.when(to == me)
        def _():
            pltpu.make_async_copy(mine.at[b], sums_ref.at[lax.rem(me, 4)], sums_recv).start()

    for s in range(5):
        whole = tiles_ref.at[pl.ds(1, 4), s]
        pltpu.make_async_copy(whole, whole, recv.at[s]).wait()

    down = device_of(lax.rem(g + 1, 8), b_me)
    up = device_of(lax.rem(g + 7, 8), b_me)
    halo_copies = []
    for k, (to, mine_at, theirs_at) in enumerate(((down, 4, 0), (up, 1, 5))):
        copy = pltpu.make_async_remote_copy(
            src_ref=tiles_ref.at[mine_at], dst_ref=tiles_ref.at[theirs_at],
            send_sem=halo_send.at[k], recv_sem=halo_recv.at[k],
            device_id={"mem": to}, device_id_type=MESH,
        )
        copy.start()
        halo_copies.append(copy)
    for s in range(5):
        some = packed.at[s, pl.ds(0, N - 1)]
        pltpu.make_async_copy(some, some, send.at[s]).wait()
    for b in range(4):
        to = device_of(me // 4, b)

        @pl.when(to != me)
        def _():
            pltpu.make_async_copy(mine.at[b], mine.at[b], sums_send.at[b]).wait()

    pltpu.make_async_copy(sums_ref, sums_ref, sums_recv).wait()
    for copy in halo_copies:
        copy.wait()


def analyse_kernel(tiles_ref, sums_ref, out_ref, anomaly, average):
    for t in range(6):
        for s in range(5):
            x = tiles_ref[t, s].astype(F32)
            mean = jnp.sum(x, axis=0, keepdims=True) * (1.0 / members)
            average[t, s : s + 1] = mean
            anomaly[t, s] = (x - mean).astype(BF16)
    diagonal = iota((256, 256), 0) == iota((256, 256), 1)
    eye = jnp.where(diagonal, 1.0, 0.0)
    for p in range(4):
        gram = (members - 1) / inflation * eye
        force = jnp.zeros((16, 256), F32)
        for dt in range(3):
            scaled, plain = [], []
            means = average[p + dt]
            weights = sums_ref[p, 0, 5 * dt : 5 * dt + 5]
            products = sums_ref[p, 1, 5 * dt : 5 * dt + 5]
            shift = split3(products - means[0:5] * weights)
            for s in range(5):
                a = anomaly[p + dt, s]
                plain.append(a)
                body = (a.astype(F32) * weights[s : s + 1]).astype(BF16)
                extra = jnp.concatenate(
                    [part[s : s + 1].astype(F32) for part in shift] + [jnp.zeros((13, 128), F32)],
                    axis=0,
                ).astype(BF16)
                scaled.append(jnp.concatenate([body, extra], axis=0))
            both = dot_nt(jnp.concatenate(scaled, axis=1), jnp.concatenate(plain, axis=1))
            gram = gram + both[0:256]
            force = force + both[256:272]
        forcing = jnp.sum(force, axis=0, keepdims=True)
        norm = jnp.sqrt(jnp.sum(jnp.sum(gram * gram, axis=0, keepdims=True), axis=1, keepdims=True))
        y = gram / norm
        y0s = split2(y)
        y1 = 1.5 * y - 0.5 * dot3(y0s, y0s)
        z1 = 1.5 * eye - 0.5 * y
        y1s = split2(y1)
        q = 1.5 * y1 - 0.5 * dot3(y0s, y1s)
        qs = split2(q)
        y2 = 1.5 * y1 - 0.5 * dot3(y1s, qs)
        z2 = 1.5 * z1 - 0.5 * dot3(qs, split2(z1))
        y2s, z2s = split2(y2), split2(z2)
        qs = split2(dot3(z2s, y2s))
        y3 = 1.5 * y2 - 0.5 * dot3(y2s, qs)
        z3 = 1.5 * z2 - 0.5 * dot3(qs, z2s)
        z3s = split2(z3)
        qs = split2(dot3(z3s, split2(y3)))
        root = 1.5 * z3 - 0.5 * dot3(qs, z3s)
        rh, rl = split2(root)

        def times_root(v):
            parts = jnp.concatenate(
                [part.astype(F32) for part in split3(v)] + [jnp.zeros((13, 256), F32)], axis=0
            ).astype(BF16)
            return jnp.sum(dot(parts, rh) + dot(parts, rl), axis=0, keepdims=True)

        mean_shift = times_root(times_root(forcing)) / norm
        transform = (jnp.sqrt((members - 1.0) / norm) * root + mean_shift).astype(BF16)
        for s in range(4):
            out = dot(transform, anomaly[p + 1, s]) + average[p + 1, s : s + 1]
            out_ref[s, p] = out.astype(BF16)


def collect_kernel(a_ref, out_ref, got, send, recv):
    me = lax.axis_index("mem")
    g, b_me = place(me)
    barrier = pltpu.get_barrier_semaphore()

    def greet(i, carry):
        pl.semaphore_signal(
            barrier, inc=1, device_id={"mem": lax.rem(me + i, N)}, device_id_type=MESH
        )
        return carry

    lax.fori_loop(1, N, greet, 0)
    pl.semaphore_wait(barrier, N - 1)

    def rows(m):
        return pl.ds(pl.multiple_of(m * 8, 8), 8)

    place_at = got.at[:, b_me, pl.ds(g * 4, 4)]
    pltpu.make_async_copy(a_ref.at[:, :, rows(me)], place_at, recv).start()

    def one(i, carry):
        to = lax.rem(me + i, N)
        pltpu.make_async_remote_copy(
            src_ref=a_ref.at[:, :, rows(to)], dst_ref=place_at,
            send_sem=send, recv_sem=recv, device_id={"mem": to}, device_id_type=MESH,
        ).start()
        return carry

    lax.fori_loop(1, N, one, 0)
    swap = swap_matrix()
    pltpu.make_async_copy(got, got, recv).wait()
    for s in range(4):
        wide = jnp.concatenate([got[s, b].reshape(256, 128) for b in range(4)], axis=1)
        out = dot(wide, swap).astype(BF16)
        for r in range(4):
            out_ref[s, r] = out[:, 128 * r : 128 * r + 128]
    some = a_ref.at[:, :, pl.ds(0, 248)]
    pltpu.make_async_copy(some, some, send).wait()


def vmem():
    return pl.BlockSpec(memory_space=pltpu.VMEM)


def params(collective_id=None):
    extra = {} if collective_id is None else {"collective_id": collective_id, "has_side_effects": True}
    return pltpu.CompilerParams(vmem_limit_bytes=48 << 20, **extra)


def local(trials, tally, cells, classes, readings, inv_var, table):
    x = trials.reshape(8, 4, 32, 4, 128).transpose(1, 3, 2, 0, 4).reshape(16, 256, 128)
    dma = pltpu.SemaphoreType.DMA
    tiles, sums = pl.pallas_call(
        spread_kernel,
        out_shape=[
            jax.ShapeDtypeStruct((6, 5, 256, 128), BF16),
            jax.ShapeDtypeStruct((4, 2, 16, 128), F32),
        ],
        in_specs=[vmem()] * 6 + [pl.BlockSpec(memory_space=pltpu.SMEM)],
        out_specs=[vmem()] * 2,
        scratch_shapes=[
            pltpu.VMEM((5, 32, 4, 8, 128), BF16),
            pltpu.VMEM((4, 2, 16, 128), F32),
            pltpu.VMEM((256, 128), BF16),
            pltpu.VMEM((2, 256, 128), BF16),
            dma((5,)), dma((5,)), dma((2,)), dma((2,)), dma((4,)), dma, dma((2,)), dma((2,)),
        ],
        compiler_params=params(0),
        name="spread",
    )(
        x,
        tally.reshape(4, 1),
        cells.reshape(4, 2048),
        classes.reshape(4, 2048),
        readings.reshape(4, 2048),
        inv_var.reshape(4, 2048),
        table,
    )
    analysed = pl.pallas_call(
        analyse_kernel,
        out_shape=jax.ShapeDtypeStruct((4, 4, 256, 128), BF16),
        in_specs=[vmem()] * 2,
        out_specs=vmem(),
        scratch_shapes=[pltpu.VMEM((6, 5, 256, 128), BF16), pltpu.VMEM((6, 8, 128), F32)],
        compiler_params=params(),
        name="analyse",
    )(tiles, sums)
    out = pl.pallas_call(
        collect_kernel,
        out_shape=jax.ShapeDtypeStruct((4, 4, 256, 128), BF16),
        in_specs=[vmem()],
        out_specs=vmem(),
        scratch_shapes=[pltpu.VMEM((4, 4, 32, 8, 128), BF16), dma, dma],
        compiler_params=params(1),
        name="collect",
    )(analysed)
    return out.reshape(4, 4, 32, 8, 128).transpose(3, 0, 2, 1, 4).reshape(8, 4, 128, 128)


def solution(mesh):
    placed = (
        P("mem", None, None, "col"),
        P("mem", "col"),
        P("mem", "col", None),
        P("mem", "col", None),
        P("mem", "col", None),
        P("mem", "col", None),
        P(),
    )
    return jax.shard_map(
        local, mesh=mesh, in_specs=placed, out_specs=P("mem", None, None, "col"), check_vma=False
    )
```
